512 devices in a mesh: seq: 64 (over x, z_hi, y, core), chan: 8 (over z_lo).
Axes of the slice: x: 4, y: 4, z: 16 (z_hi: 2, z_lo: 8; z = z_hi * 8 + z_lo), core: 2. Of those that a mesh axis runs over, the one named last changes fastest.
Arguments:
- q_proj: float32 [8192, 4096], P('seq', 'chan'), may hold values from -6 to 6
- k_proj: float32 [8192, 4096], P('seq', 'chan'), may hold values from -6 to 6
- v_proj: float32 [8192, 4096], P('seq', 'chan'), may hold values from -6 to 6
- taps: float32 [512, 4, 128], P(('seq', 'chan')), may hold values from -0.25 to 0.25
- skip_bias: float32 [4096], P('chan'), may hold values from -1 to 1
- group_index: int32 [4096], P('chan'), may hold values from 0 to 511
- offsets: int32 [4], replicated, may hold values from 0 to 63
Outputs:
- mixed: float32 [8192, 4096], P('seq', 'chan')
The draws below stay inside these ranges and needn't reach their ends.
All inputs are finite; a program needn't handle non-finite values.
Results may differ from the reference program's by a relative error of at most 0.000054.
Values sent between devices are 32-bit elements; how exact they have to be, the bound alone decides.
A program may use at most 64 MiB of HBM per device.

```python
import jax
import jax.numpy as jnp
from jax import lax

WIDTH = 4096
GROUPS = 512
LAGS = 4
TOK_DEV = 128
SEQ = 8192
N_SEQ = 64


def set_ends(values, key, low, high):
    index_at = [jax.random.randint(jax.random.fold_in(key, axis), (), 0, length) for axis, length in enumerate(values.shape)]
    longest = values.shape.index(max(values.shape))
    beside = index_at[:longest] + [(index_at[longest] + 1) % values.shape[longest]] + index_at[longest + 1:]
    return values.at[tuple(index_at)].set(low).at[tuple(beside)].set(high)


def steps_of(rng, dims, shards, least, largest):
    loudness = 1.0
    for position, shards_of in shards:
        heights = jax.random.uniform(jax.random.fold_in(jax.random.fold_in(rng, 6), position), (shards_of,), jnp.float32, least / len(shards), largest / len(shards))
        loudness = loudness * jnp.repeat(jnp.exp(heights), dims[position] // shards_of).reshape((-1,) + (1,) * (len(dims) - 1 - position))
    return loudness


def noise(rng, dims, width, limit, split=(), held_as=jnp.bfloat16):
    array = width * jax.random.normal(rng, dims, jnp.float32)
    if split:
        array = array * steps_of(rng, dims, split, -0.22, 0.18)
    return jnp.clip(array, -limit, limit).astype(held_as)


def setup_inputs(seed: int = 0) -> dict:
    streams_of = jax.random.split(jax.random.key(seed), 8)
    q_proj = noise(streams_of[0], (SEQ, WIDTH), 1.0, 6.0, ((0, 64), (1, 8)), jnp.float32)
    k_proj = noise(streams_of[1], (SEQ, WIDTH), 1.0, 6.0, ((0, 64), (1, 8)), jnp.float32)
    v_proj = noise(streams_of[2], (SEQ, WIDTH), 1.0, 6.0, ((0, 64), (1, 8)), jnp.float32)
    taps = noise(streams_of[3], (GROUPS, LAGS, TOK_DEV), (LAGS * TOK_DEV) ** -0.5, 0.25, ((0, 512),), jnp.float32)
    skip_bias = jnp.clip(jax.random.uniform(streams_of[4], (WIDTH,), jnp.float32, -1.0, 1.0) * steps_of(streams_of[4], (WIDTH,), ((0, 8),), -0.4, 0.0), -1.0, 1.0)
    group_index = set_ends(jax.random.randint(streams_of[5], (WIDTH,), 0, GROUPS), jax.random.fold_in(streams_of[5], 1), 0, GROUPS - 1).astype(jnp.int32)
    offsets = set_ends(jax.random.randint(streams_of[6], (LAGS,), 0, N_SEQ), jax.random.fold_in(streams_of[6], 1), 0, N_SEQ - 1).astype(jnp.int32)
    return {"q_proj": q_proj, "k_proj": k_proj, "v_proj": v_proj, "taps": taps, "skip_bias": skip_bias, "group_index": group_index, "offsets": offsets}


def reference(q_proj, k_proj, v_proj, taps, skip_bias, group_index, offsets):
    gated_in = k_proj * v_proj
    lag_pos = (offsets[:, None] * TOK_DEV + jnp.arange(TOK_DEV, dtype=jnp.int32)[None, :]).astype(jnp.int32)
    filters_full = jnp.zeros((GROUPS, SEQ), dtype=taps.dtype)
    filters_full = filters_full.at[:, lag_pos.reshape(-1)].add(taps.reshape(GROUPS, LAGS * TOK_DEV), mode="drop")
    filter_spec = jnp.fft.rfft(filters_full, n=2 * SEQ, axis=1)
    chan_block = 256 if WIDTH % 256 == 0 else WIDTH
    block_count = WIDTH // chan_block
    inputs_t = gated_in.T.reshape(block_count, chan_block, SEQ)
    groups_b = group_index.reshape(block_count, chan_block)

    def convolve_block(pair):
        block_in, block_group = pair
        input_spec = jnp.fft.rfft(block_in, n=2 * SEQ, axis=1)
        result = jnp.fft.irfft(input_spec * filter_spec[block_group], n=2 * SEQ, axis=1)
        return result[:, :SEQ].astype(gated_in.dtype)

    convolved = lax.map(convolve_block, (inputs_t, groups_b)).reshape(WIDTH, SEQ).T
    return q_proj * (convolved + skip_bias[None, :] * gated_in)
```

```python
import functools

import jax
import jax.numpy as jnp
from jax import lax
from jax.experimental import pallas as pl
from jax.experimental.pallas import tpu as pltpu
from jax.sharding import PartitionSpec as P


def split(x):
    hi = x.astype(jnp.bfloat16)
    lo = (x - hi.astype(jnp.float32)).astype(jnp.bfloat16)
    return hi, lo


def dot(a, b):
    return jnp.dot(a, b, preferred_element_type=jnp.float32)


def conv_kernel(groups_ref, offsets_ref, x_ref, taps_ref, y_ref, padded, toep_hi, toep_lo):
    blocks, channels, width = x_ref.shape
    lags = taps_ref.shape[1]
    padded[:blocks] = jnp.zeros((blocks, width), jnp.float32)
    for c in range(channels):
        padded[blocks:] = x_ref[:, c, :]
        filt = taps_ref[groups_ref[c]]
        parts = []
        for k in range(lags):
            parts.append(padded[pl.ds(blocks - offsets_ref[k], blocks), :])
            row = jnp.concatenate([filt[k : k + 1], jnp.zeros((1, width), jnp.float32)], axis=1)
            rows = jnp.broadcast_to(row, (width, 2 * width))
            toep = pltpu.roll(rows, 0, 1, stride=1, stride_axis=0)
            hi, lo = split(toep)
            toep_hi[k * width : (k + 1) * width] = hi
            toep_lo[k * width : (k + 1) * width] = lo
        hi, lo = split(jnp.concatenate(parts, axis=1))
        y = dot(hi, toep_hi[...]) + dot(lo, toep_hi[...]) + dot(hi, toep_lo[...])
        tail = jnp.concatenate([jnp.zeros((1, width), jnp.float32), y[: blocks - 1, width:]], axis=0)
        y_ref[:, c, :] = y[:, :width] + tail


def convolve(x, taps, groups, offsets):
    lags, width = taps.shape[1:]
    smem = pl.BlockSpec(memory_space=pltpu.SMEM)
    vmem = pl.BlockSpec(memory_space=pltpu.VMEM)
    return pl.pallas_call(
        conv_kernel,
        out_shape=jax.ShapeDtypeStruct(x.shape, jnp.float32),
        in_specs=[smem, smem, vmem, vmem],
        out_specs=vmem,
        scratch_shapes=[
            pltpu.VMEM((2 * x.shape[0], width), jnp.float32),
            pltpu.VMEM((lags * width, 2 * width), jnp.bfloat16),
            pltpu.VMEM((lags * width, 2 * width), jnp.bfloat16),
        ],
    )(groups, offsets, x, taps)


def local(q_proj, k_proj, v_proj, taps, skip_bias, group_index, offsets):
    gated_in = k_proj * v_proj
    block_len, chans = gated_in.shape
    seq = lax.axis_size("seq")
    share = chans // seq
    run_taps = lax.all_gather(taps, "chan", axis=0, tiled=True)
    all_taps = lax.all_gather(run_taps, "seq", axis=0, tiled=True)
    sent = gated_in.T.reshape(seq, share, block_len)
    x = lax.all_to_all(sent, "seq", 0, 0, tiled=True)
    groups = lax.dynamic_slice(group_index, (lax.axis_index("seq") * share,), (share,))
    y = convolve(x, all_taps, groups, offsets)
    back = lax.all_to_all(y, "seq", 0, 0, tiled=True)
    convolved = back.reshape(chans, block_len).T
    return q_proj * (convolved + skip_bias[None, :] * gated_in)


def solution(mesh):
    return jax.shard_map(
        local,
        mesh=mesh,
        in_specs=(
            P("seq", "chan"),
            P("seq", "chan"),
            P("seq", "chan"),
            P(("seq", "chan"), None, None),
            P("chan"),
            P("chan"),
            P(),
        ),
        out_specs=P("seq", "chan"),
        check_vma=False,
    )
```

```python
import functools

import jax
import jax.numpy as jnp
from jax import lax
from jax.experimental import pallas as pl
from jax.experimental.pallas import tpu as pltpu
from jax.sharding import PartitionSpec as P

MESH = pl.DeviceIdType.MESH
SUBS = 2


def split(x):
    hi = x.astype(jnp.bfloat16)
    lo = (x - hi.astype(jnp.float32)).astype(jnp.bfloat16)
    return hi, lo


def dot(a, b):
    return jnp.dot(a, b, preferred_element_type=jnp.float32)


def kernel(
    groups_ref,
    offsets_ref,
    q_ref,
    k_ref,
    v_ref,
    bias_ref,
    taps_ref,
    o_ref,
    sent,
    tiles,
    ring,
    padded,
    toep_hi,
    toep_lo,
    result,
    returned,
    column,
    table,
    tile_send,
    tile_recv,
    ring_send,
    ring_recv,
    tap_send,
    tap_recv,
    table_send,
    table_recv,
    back_send,
    back_recv,
):
    width = k_ref.shape[0]
    lags = taps_ref.shape[1]
    plane = tiles.shape[0]
    depth = column.shape[0]
    inner = 8
    slabs = plane // inner
    hops = depth // 2
    blocks = 2 * plane
    s = lax.axis_index("seq")
    j = lax.axis_index("chan")
    half = (s // inner) % 2
    p = (s // (2 * inner)) * inner + s % inner
    z = half * hops + j

    def at_plane(i):
        other = (p + i) % plane
        return other, {"seq": (other // inner) * 2 * inner + half * inner + other % inner}

    def at_z(step):
        there = (z + step + depth) % depth
        return {"seq": s + inner * (there // hops - half), "chan": there % hops}

    barrier = pltpu.get_barrier_semaphore()

    def greet(i, carry):
        _, device = at_plane(i)
        pl.semaphore_signal(barrier, inc=1, device_id=device, device_id_type=MESH)
        return carry

    for step in (1, -1):
        pl.semaphore_signal(barrier, inc=1, device_id=at_z(step), device_id_type=MESH)
    lax.fori_loop(1, plane, greet, 0)

    column[z] = taps_ref[0]
    for i in range(slabs):
        cols = slice(i * 128, (i + 1) * 128)
        turned = (k_ref[:, cols] * v_ref[:, cols]).T
        sent[i * inner : (i + 1) * inner] = turned.reshape(inner, SUBS, 8, width)
    padded[:, :blocks] = jnp.zeros((padded.shape[0], blocks, width), jnp.float32)
    pl.semaphore_wait(barrier, plane - 1 + 2)

    def tile_copy(i):
        other, device = at_plane(i)
        return pltpu.make_async_remote_copy(
            src_ref=sent.at[other],
            dst_ref=tiles.at[p],
            send_sem=tile_send,
            recv_sem=tile_recv,
            device_id=device,
            device_id_type=MESH,
        )

    def table_copy(i):
        _, device = at_plane(i)
        return pltpu.make_async_remote_copy(
            src_ref=column,
            dst_ref=table.at[pl.ds(p * depth, depth)],
            send_sem=table_send,
            recv_sem=table_recv,
            device_id=device,
            device_id_type=MESH,
        )

    def back_copy(i, sub):
        other, device = at_plane(i)
        return pltpu.make_async_remote_copy(
            src_ref=result.at[other, sub],
            dst_ref=returned.at[p, sub],
            send_sem=back_send.at[sub],
            recv_sem=back_recv.at[sub],
            device_id=device,
            device_id_type=MESH,
        )

    def start_all(copy):
        def start(i, carry):
            copy(i).start()
            return carry

        lax.fori_loop(1, plane, start, 0)

    def wait_bytes(ref, sem):
        pltpu.make_async_copy(ref, ref, sem).wait()

    def tap_copy(hop, way):
        origin = (z - (hop - 1) * (1, -1)[way] + depth) % depth
        return pltpu.make_async_remote_copy(
            src_ref=column.at[origin],
            dst_ref=column.at[origin],
            send_sem=tap_send.at[way, hop - 1],
            recv_sem=tap_recv.at[way, hop - 1],
            device_id=at_z((1, -1)[way]),
            device_id_type=MESH,
        )

    def ring_copy(hop, way, sub):
        return pltpu.make_async_remote_copy(
            src_ref=ring.at[way, hop - 1, sub],
            dst_ref=ring.at[way, hop, sub],
            send_sem=ring_send.at[way, hop - 1, sub],
            recv_sem=ring_recv.at[way, hop - 1, sub],
            device_id=at_z((1, -1)[way]),
            device_id_type=MESH,
        )

    def tap_hop(hop):
        for way in (0, 1):
            if hop > 1 and hop - 1 <= hops - way:
                tap_copy(hop - 1, way).wait_recv()
            if hop <= hops - way:
                tap_copy(hop, way).start()

    def ring_hop(hop, sub):
        for way in (0, 1):
            ring_copy(hop - 1, way, sub).wait_recv()
            ring_copy(hop, way, sub).start()

    start_all(tile_copy)
    tiles[p] = sent[p]
    for hop in range(1, 5):
        tap_hop(hop)

    wait_bytes(tiles.at[pl.ds(0, plane - 1)], tile_recv)
    chans = padded.shape[0]
    for c in range(chans):
        sub, way, i = c // 8, (c % 8) // 4, c % 4
        x = tiles[:, sub, c % 8, :]
        ring[way, 0, sub, i] = x
        for m in range(slabs):
            padded[c, pl.ds(pl.multiple_of(blocks + m * 2 * inner + half * inner, 8), inner), :] = x[m * inner : (m + 1) * inner]
    for sub in range(SUBS):
        for way in (0, 1):
            ring_copy(1, way, sub).start()

    for hop in range(5, hops + 2):
        tap_hop(hop)
    start_all(table_copy)
    table[pl.ds(p * depth, depth)] = column[...]

    def ring_step(hop, carry):
        for sub in range(SUBS):
            ring_hop(hop, sub)
        return carry

    lax.fori_loop(2, hops - 1, ring_step, 0)

    def toeplitz(c, carry):
        group = groups_ref[p * chans + c]
        owner = group // hops
        row = ((owner // (2 * inner)) * inner + owner % inner) * depth + ((owner // inner) % 2) * hops + group % hops
        filt = table[row]
        for lag in range(lags):
            line = jnp.concatenate([filt[lag : lag + 1], jnp.zeros((1, width), jnp.float32)], axis=1)
            lines = jnp.broadcast_to(line, (width, 2 * width))
            hi, lo = split(pltpu.roll(lines, 0, 1, stride=1, stride_axis=0))
            toep_hi[c, lag * width : (lag + 1) * width] = hi
            toep_lo[c, lag * width : (lag + 1) * width] = lo
        return carry

    wait_bytes(table.at[pl.ds(0, (plane - 1) * depth)], table_recv)
    piece = chans // (2 * SUBS)
    for hop in (hops - 1, hops):
        for sub in range(SUBS):
            ring_hop(hop, sub)
            first = ((hop - hops + 1) * SUBS + sub) * piece
            lax.fori_loop(first, first + piece, toeplitz, 0)

    def convolve(c, carry):
        sub, way, i = c // 8, (c % 8) // 4, c % 4
        x = ring[way, hops, sub, i]
        for m in range(slabs):
            padded[c, pl.ds(pl.multiple_of(blocks + m * 2 * inner + (1 - half) * inner, 8), inner), :] = x[m * inner : (m + 1) * inner]
        parts = [padded[c, pl.ds(blocks - offsets_ref[lag], blocks), :] for lag in range(lags)]
        hi, lo = split(jnp.concatenate(parts, axis=1))
        y = dot(hi, toep_hi[c]) + dot(lo, toep_hi[c]) + dot(hi, toep_lo[c])
        tail = jnp.concatenate([jnp.zeros((1, width), jnp.float32), y[: blocks - 1, width:]], axis=0)
        total = y[:, :width] + tail
        for m in range(slabs):
            low = total[m * 2 * inner : m * 2 * inner + inner]
            high = total[m * 2 * inner + inner : (m + 1) * 2 * inner]
            result[m * inner : (m + 1) * inner, sub, c % 8, :] = jnp.where(half == 0, low, high)
        return carry

    for sub in range(SUBS):
        for way in (0, 1):
            ring_copy(hops, way, sub).wait_recv()
        lax.fori_loop(sub * 8, (sub + 1) * 8, convolve, 0)
        start_all(functools.partial(back_copy, sub=sub))
    returned[p] = result[p]

    def drain(hop, carry):
        for sub in range(SUBS):
            for way in (0, 1):
                ring_copy(hop, way, sub).wait_send()
        return carry

    lax.fori_loop(1, hops + 1, drain, 0)
    for way in (0, 1):
        for hop in range(1, hops + 1 - way):
            tap_copy(hop, way).wait_send()
    wait_bytes(sent.at[pl.ds(0, plane - 1)], tile_send)
    wait_bytes(table.at[pl.ds(0, (plane - 1) * depth)], table_send)
    for sub in range(SUBS):
        wait_bytes(result.at[pl.ds(0, plane - 1), 0], back_send.at[sub])
    for sub in range(SUBS):
        wait_bytes(returned.at[pl.ds(0, plane - 1), 0], back_recv.at[sub])
    for i in range(slabs):
        cols = slice(i * 128, (i + 1) * 128)
        convolved = returned[i * inner : (i + 1) * inner].reshape(128, width).T
        gated = k_ref[:, cols] * v_ref[:, cols]
        o_ref[:, cols] = q_ref[:, cols] * (convolved + bias_ref[:, cols] * gated)


def local(q_proj, k_proj, v_proj, taps, skip_bias, group_index, offsets):
    width, chans = k_proj.shape
    lags = taps.shape[1]
    seq = lax.axis_size("seq")
    chan = lax.axis_size("chan")
    plane, depth = seq // 2, 2 * chan
    share = chans // plane
    smem = pl.BlockSpec(memory_space=pltpu.SMEM)
    vmem = pl.BlockSpec(memory_space=pltpu.VMEM)
    f32, b16, dma = jnp.float32, jnp.bfloat16, pltpu.SemaphoreType.DMA
    return pl.pallas_call(
        kernel,
        out_shape=jax.ShapeDtypeStruct((width, chans), f32),
        in_specs=[smem, smem, vmem, vmem, vmem, vmem, vmem],
        out_specs=vmem,
        scratch_shapes=[
            pltpu.VMEM((plane, SUBS, 8, width), f32),
            pltpu.VMEM((plane, SUBS, 8, width), f32),
            pltpu.VMEM((2, chan + 1, SUBS, 4, plane, width), f32),
            pltpu.VMEM((share, 2 * seq, width), f32),
            pltpu.VMEM((share, lags * width, 2 * width), b16),
            pltpu.VMEM((share, lags * width, 2 * width), b16),
            pltpu.VMEM((plane, SUBS, 8, width), f32),
            pltpu.VMEM((plane, SUBS, 8, width), f32),
            pltpu.VMEM((depth, lags, width), f32),
            pltpu.VMEM((plane * depth, lags, width), f32),
            dma(()),
            dma(()),
            dma((2, chan, SUBS)),
            dma((2, chan, SUBS)),
            dma((2, chan)),
            dma((2, chan)),
            dma(()),
            dma(()),
            dma((SUBS,)),
            dma((SUBS,)),
        ],
        compiler_params=pltpu.CompilerParams(collective_id=0, has_side_effects=True, vmem_limit_bytes=60 << 20),
    )(group_index, offsets, q_proj, k_proj, v_proj, skip_bias[None, :], taps)


def solution(mesh):
    return jax.shard_map(
        local,
        mesh=mesh,
        in_specs=(
            P("seq", "chan"),
            P("seq", "chan"),
            P("seq", "chan"),
            P(("seq", "chan"), None, None),
            P("chan"),
            P("chan"),
            P(),
        ),
        out_specs=P("seq", "chan"),
        check_vma=False,
    )
```

```python
import functools

import jax
import jax.numpy as jnp
from jax import lax
from jax.experimental import pallas as pl
from jax.experimental.pallas import tpu as pltpu
from jax.sharding import PartitionSpec as P

MESH = pl.DeviceIdType.MESH
SUBS = 2
PIECES = 2


def split(x):
    hi = x.astype(jnp.bfloat16)
    lo = (x - hi.astype(jnp.float32)).astype(jnp.bfloat16)
    return hi, lo


def dot(a, b):
    return jnp.dot(a, b, preferred_element_type=jnp.float32)


def kernel(
    groups_ref,
    offsets_ref,
    q_hbm,
    k_hbm,
    v_hbm,
    bias_ref,
    taps_hbm,
    o_ref,
    q_ref,
    k_ref,
    v_ref,
    sent,
    tiles,
    raw,
    foreign,
    ring,
    padded,
    toep_hi,
    toep_lo,
    result,
    returned,
    column,
    table,
    load_sem,
    tile_send,
    tile_recv,
    raw_send,
    raw_recv,
    foreign_send,
    foreign_recv,
    ring_send,
    ring_recv,
    tap_send,
    tap_recv,
    table_send,
    table_recv,
    back_send,
    back_recv,
):
    width = k_ref.shape[0]
    lags = taps_hbm.shape[1]
    plane = tiles.shape[1]
    depth = column.shape[0]
    chans = padded.shape[0]
    inner = 8
    slabs = plane // inner
    hops = depth // 2
    blocks = 2 * plane
    early = hops + 1
    s = lax.axis_index("seq")
    j = lax.axis_index("chan")
    half = (s // inner) % 2
    p = (s // (2 * inner)) * inner + s % inner
    z = half * hops + j

    def at_plane(i):
        other = (p + i) % plane
        return other, {"seq": (other // inner) * 2 * inner + half * inner + other % inner}

    def at_z(step):
        there = (z + step + depth) % depth
        return {"seq": s + inner * (there // hops - half), "chan": there % hops}

    loads = [
        pltpu.make_async_copy(src, dst, load_sem.at[i])
        for i, (src, dst) in enumerate(((k_hbm, k_ref), (v_hbm, v_ref), (taps_hbm.at[0], column.at[0]), (q_hbm, q_ref)))
    ]
    for load in loads:
        load.start()
    barrier = pltpu.get_barrier_semaphore()

    def greet(i, carry):
        _, device = at_plane(i)
        pl.semaphore_signal(barrier, inc=1, device_id=device, device_id_type=MESH)
        return carry

    for step in (1, -1):
        pl.semaphore_signal(barrier, inc=1, device_id=at_z(step), device_id_type=MESH)
    lax.fori_loop(1, plane, greet, 0)

    for load in loads:
        load.wait()
    for i in range(slabs):
        cols = slice(i * 128, (i + 1) * 128)
        turned = (k_ref[:, cols] * v_ref[:, cols]).T.reshape(inner, SUBS, 8, width)
        for sub in range(SUBS):
            sent[sub, i * inner : (i + 1) * inner] = turned[:, sub]
    padded[:, :blocks] = jnp.zeros((chans, blocks, width), jnp.float32)
    pl.semaphore_wait(barrier, plane - 1 + 2)

    def plane_copy(i, src, dst, send_sem, recv_sem):
        return pltpu.make_async_remote_copy(
            src_ref=src,
            dst_ref=dst,
            send_sem=send_sem,
            recv_sem=recv_sem,
            device_id=at_plane(i)[1],
            device_id_type=MESH,
        )

    def z_copy(way, src, dst, send_sem, recv_sem):
        return pltpu.make_async_remote_copy(
            src_ref=src,
            dst_ref=dst,
            send_sem=send_sem,
            recv_sem=recv_sem,
            device_id=at_z((1, -1)[way]),
            device_id_type=MESH,
        )

    def tile_copy(i):
        return plane_copy(i, sent.at[:, at_plane(i)[0]], tiles.at[:, p], tile_send, tile_recv)

    def table_copy(i, part):
        first, size = ((0, early), (early, depth - early))[part]
        src, dst = column.at[pl.ds(first, size)], table.at[pl.ds(p * depth + first, size)]
        return plane_copy(i, src, dst, table_send.at[part], table_recv.at[part])

    def foreign_copy(i):
        other = at_plane(i)[0]
        src = raw.at[other // (plane // 2), hops - 1, other % (plane // 2)]
        return plane_copy(i, src, foreign.at[p], foreign_send, foreign_recv)

    def back_copy(i, sub):
        return plane_copy(i, result.at[sub, at_plane(i)[0]], returned.at[sub, p], back_send.at[sub], back_recv.at[sub])

    def start_all(copy):
        def start(i, carry):
            copy(i).start()
            return carry

        lax.fori_loop(1, plane, start, 0)

    def wait_bytes(ref, sem):
        pltpu.make_async_copy(ref, ref, sem).wait()

    def place(hop, way):
        return 2 * hop - 1 + way if hop else 0

    def tap_copy(hop, way):
        src, dst = column.at[place(hop - 1, way)], column.at[place(hop, way)]
        return z_copy(way, src, dst, tap_send.at[way, hop - 1], tap_recv.at[way, hop - 1])

    def raw_copy(hop, way, piece):
        size = plane // 2 // PIECES
        src = sent.at[0, pl.ds(way * (plane // 2) + piece * size, size)] if hop == 1 else raw.at[way, hop - 2, pl.ds(piece * size, size)]
        dst = raw.at[way, hop - 1, pl.ds(piece * size, size)]
        return z_copy(way, src, dst, raw_send.at[way, hop - 1, piece], raw_recv.at[way, hop - 1, piece])

    def ring_copy(hop, way, piece):
        src, dst = ring.at[way, hop - 1, piece], ring.at[way, hop, piece]
        return z_copy(way, src, dst, ring_send.at[way, hop - 1, piece], ring_recv.at[way, hop - 1, piece])

    def tap_hop(hop):
        for way in (0, 1):
            if 1 < hop <= hops + 1 - way:
                tap_copy(hop - 1, way).wait_recv()
            if hop <= hops - way:
                tap_copy(hop, way).start()

    def hop_pieces(copy, hop):
        for piece in range(PIECES):
            for way in (0, 1):
                if hop > 1:
                    copy(hop - 1, way, piece).wait_recv()
                if hop <= hops:
                    copy(hop, way, piece).start()

    def own_rows(c, x, side):
        for m in range(slabs):
            row = pl.multiple_of(blocks + m * 2 * inner + side * inner, 8)
            padded[c, pl.ds(row, inner), :] = x[m * inner : (m + 1) * inner]

    tap_hop(1)
    hop_pieces(raw_copy, 1)
    start_all(tile_copy)
    tiles[:, p] = sent[:, p]
    tap_hop(2)
    hop_pieces(raw_copy, 2)
    tap_hop(3)
    hop_pieces(raw_copy, 3)
    tap_hop(4)
    wait_bytes(tiles.at[:, pl.ds(0, plane - 1)], tile_recv)
    for cc in range(8):
        x = tiles[1, :, cc, :]
        ring[cc // 4, 0, cc % 4 // (4 // PIECES), cc % (4 // PIECES)] = x
        own_rows(8 + cc, x, half)
    hop_pieces(ring_copy, 1)
    tap_hop(5)
    hop_pieces(raw_copy, 4)
    start_all(functools.partial(table_copy, part=0))
    tap_hop(6)
    hop_pieces(ring_copy, 2)
    hop_pieces(raw_copy, 5)
    tap_hop(7)
    hop_pieces(ring_copy, 3)
    tap_hop(8)
    hop_pieces(raw_copy, 6)
    tap_hop(9)
    start_all(functools.partial(table_copy, part=1))
    hop_pieces(ring_copy, 4)
    table[pl.ds(p * depth, depth)] = column[...]
    for cc in range(8):
        own_rows(cc, tiles[0, :, cc, :], half)
    hop_pieces(raw_copy, 7)
    hop_pieces(ring_copy, 5)
    hop_pieces(raw_copy, 8)
    hop_pieces(ring_copy, 6)
    hop_pieces(raw_copy, 9)
    start_all(foreign_copy)
    foreign[p] = raw[p // (plane // 2), hops - 1, p % (plane // 2)]
    hop_pieces(ring_copy, 7)
    row_at = lax.broadcasted_iota(jnp.int32, (width, width), 0)
    col_at = lax.broadcasted_iota(jnp.int32, (width, width), 1)
    same = col_at >= row_at
    none = jnp.zeros((width, width), jnp.bfloat16)

    def toeplitz(c, carry):
        group = groups_ref[p * chans + c]
        owner = group // hops
        away = ((owner // inner) % 2 * hops + group % hops - z + depth) % depth
        slot = jnp.where(away < hops, 2 * away, 2 * (depth - away) - 1)
        filt = table[((owner // (2 * inner)) * inner + owner % inner) * depth + slot]
        for lag in range(lags):
            lines = jnp.broadcast_to(filt[lag : lag + 1], (width, width))
            rows = slice(lag * width, (lag + 1) * width)
            for part, held in zip(split(pltpu.roll(lines, 0, 1, stride=1, stride_axis=0)), (toep_hi, toep_lo)):
                held[c, rows, :width] = jnp.where(same, part, none)
                held[c, rows, width:] = jnp.where(same, none, part)
        return carry

    wait_bytes(table.at[pl.ds(0, (plane - 1) * early)], table_recv.at[0])
    wait_bytes(table.at[pl.ds(0, (plane - 1) * (depth - early))], table_recv.at[1])
    lax.fori_loop(0, 8, toeplitz, 0, unroll=4)
    hop_pieces(ring_copy, 8)
    lax.fori_loop(8, 16, toeplitz, 0, unroll=4)

    def convolve(c, x):
        own_rows(c, x, 1 - half)
        parts = [padded[c, pl.ds(blocks - offsets_ref[lag], blocks), :] for lag in range(lags)]
        hi, lo = split(jnp.concatenate(parts, axis=1))
        both = dot(jnp.concatenate([hi, lo], axis=0), toep_hi[c])
        y = both[:blocks] + both[blocks:] + dot(hi, toep_lo[c])
        tail = jnp.concatenate([jnp.zeros((1, width), jnp.float32), y[: blocks - 1, width:]], axis=0)
        total = y[:, :width] + tail
        for m in range(slabs):
            low = total[m * 2 * inner : m * 2 * inner + inner]
            high = total[m * 2 * inner + inner : (m + 1) * 2 * inner]
            result[c // 8, m * inner : (m + 1) * inner, c % 8, :] = jnp.where(half == 0, low, high)

    wait_bytes(foreign.at[pl.ds(0, plane - 1)], foreign_recv)
    for cc in range(8):
        convolve(cc, foreign[:, cc, :])
    start_all(functools.partial(back_copy, sub=0))
    returned[0, p] = result[0, p]
    for piece in range(PIECES):
        for way in (0, 1):
            ring_copy(hops, way, piece).wait_recv()
        size = 4 // PIECES
        for way in (0, 1):
            for i in range(size):
                convolve(8 + way * 4 + piece * size + i, ring[way, hops, piece, i])
    start_all(functools.partial(back_copy, sub=1))
    returned[1, p] = result[1, p]
    for hop in range(1, hops + 1):
        for way in (0, 1):
            for piece in range(PIECES):
                raw_copy(hop, way, piece).wait_send()
                ring_copy(hop, way, piece).wait_send()
            if hop <= hops - way:
                tap_copy(hop, way).wait_send()
    wait_bytes(sent.at[:, pl.ds(0, plane - 1)], tile_send)
    wait_bytes(foreign.at[pl.ds(0, plane - 1)], foreign_send)
    wait_bytes(table.at[pl.ds(0, (plane - 1) * early)], table_send.at[0])
    wait_bytes(table.at[pl.ds(0, (plane - 1) * (depth - early))], table_send.at[1])
    for sub in range(SUBS):
        wait_bytes(result.at[sub, pl.ds(0, plane - 1)], back_send.at[sub])
    for sub in range(SUBS):
        wait_bytes(returned.at[sub, pl.ds(0, plane - 1)], back_recv.at[sub])
    for i in range(slabs):
        cols = slice(i * 128, (i + 1) * 128)
        halves = [returned[sub, i * inner : (i + 1) * inner] for sub in range(SUBS)]
        convolved = jnp.stack(halves, axis=1).reshape(128, width).T
        gated = k_ref[:, cols] * v_ref[:, cols]
        o_ref[:, cols] = q_ref[:, cols] * (convolved + bias_ref[:, cols] * gated)


def local(q_proj, k_proj, v_proj, taps, skip_bias, group_index, offsets):
    width, chans = k_proj.shape
    lags = taps.shape[1]
    seq = lax.axis_size("seq")
    chan = lax.axis_size("chan")
    plane, depth = seq // 2, 2 * chan
    share = chans // plane
    smem = pl.BlockSpec(memory_space=pltpu.SMEM)
    vmem = pl.BlockSpec(memory_space=pltpu.VMEM)
    hbm = pl.BlockSpec(memory_space=pl.ANY)
    f32, b16, dma = jnp.float32, jnp.bfloat16, pltpu.SemaphoreType.DMA
    return pl.pallas_call(
        kernel,
        out_shape=jax.ShapeDtypeStruct((width, chans), f32),
        in_specs=[smem, smem, hbm, hbm, hbm, vmem, hbm],
        out_specs=vmem,
        scratch_shapes=[
            pltpu.VMEM((width, chans), f32),
            pltpu.VMEM((width, chans), f32),
            pltpu.VMEM((width, chans), f32),
            pltpu.VMEM((SUBS, plane, 8, width), f32),
            pltpu.VMEM((SUBS, plane, 8, width), f32),
            pltpu.VMEM((2, chan, plane // 2, 8, width), f32),
            pltpu.VMEM((plane, 8, width), f32),
            pltpu.VMEM((2, chan + 1, PIECES, 4 // PIECES, plane, width), f32),
            pltpu.VMEM((share, 2 * seq, width), f32),
            pltpu.VMEM((share, lags * width, 2 * width), b16),
            pltpu.VMEM((share, lags * width, 2 * width), b16),
            pltpu.VMEM((SUBS, plane, 8, width), f32),
            pltpu.VMEM((SUBS, plane, 8, width), f32),
            pltpu.VMEM((depth, lags, width), f32),
            pltpu.VMEM((plane * depth, lags, width), f32),
            dma((4,)),
            dma(()),
            dma(()),
            dma((2, chan, PIECES)),
            dma((2, chan, PIECES)),
            dma(()),
            dma(()),
            dma((2, chan, PIECES)),
            dma((2, chan, PIECES)),
            dma((2, chan)),
            dma((2, chan)),
            dma((2,)),
            dma((2,)),
            dma((SUBS,)),
            dma((SUBS,)),
        ],
        compiler_params=pltpu.CompilerParams(collective_id=0, has_side_effects=True, vmem_limit_bytes=60 << 20),
    )(group_index, offsets, q_proj, k_proj, v_proj, skip_bias[None, :], taps)


def solution(mesh):
    return jax.shard_map(
        local,
        mesh=mesh,
        in_specs=(
            P("seq", "chan"),
            P("seq", "chan"),
            P("seq", "chan"),
            P(("seq", "chan"), None, None),
            P("chan"),
            P("chan"),
            P(),
        ),
        out_specs=P("seq", "chan"),
        check_vma=False,
    )
```

```python
import functools

import jax
import jax.numpy as jnp
from jax import lax
from jax.experimental import pallas as pl
from jax.experimental.pallas import tpu as pltpu
from jax.sharding import PartitionSpec as P

MESH = pl.DeviceIdType.MESH
RAW = 4
RAW_PIECES = 1
PIECES = 4
BATCHES = 4


def split(x):
    hi = x.astype(jnp.bfloat16)
    lo = (x - hi.astype(jnp.float32)).astype(jnp.bfloat16)
    return hi, lo


def dot(a, b):
    return jnp.dot(a, b, preferred_element_type=jnp.float32)


def kernel(
    groups_hbm,
    offsets_hbm,
    q_hbm,
    k_hbm,
    v_hbm,
    bias_hbm,
    taps_hbm,
    o_ref,
    groups_ref,
    offsets_ref,
    q_ref,
    k_ref,
    v_ref,
    bias_ref,
    sent,
    tiles,
    raw,
    foreign,
    mine,
    far,
    padded,
    toep_hi,
    toep_lo,
    result,
    returned,
    column,
    table,
    load_sem,
    tile_send,
    tile_recv,
    raw_send,
    raw_recv,
    foreign_send,
    foreign_recv,
    far_send,
    far_recv,
    tap_send,
    tap_recv,
    table_send,
    table_recv,
    own_sem,
    twin_send,
    twin_recv,
    back_send,
    back_recv,
):
    width = k_ref.shape[0]
    lags = taps_hbm.shape[1]
    plane = tiles.shape[0]
    depth = column.shape[0]
    chans = padded.shape[0]
    chips = plane // 2
    batch = chans // BATCHES
    size = (chans - RAW) // PIECES
    inner = 8
    slabs = plane // inner
    chan = depth // 2
    blocks = 2 * plane
    s = lax.axis_index("seq")
    j = lax.axis_index("chan")
    half = (s // inner) % 2
    p = (s // (2 * inner)) * inner + s % inner
    z = half * chan + j

    mine_x, mine_y, core = p // inner, p // 2 % (inner // 2), p % 2

    def at_plane(step):
        right, up, other = step
        x, there = (mine_x + right) % slabs, (mine_y + up) % (inner // 2) * 2 + (core + other) % 2
        return x * inner + there, {"seq": x * 2 * inner + half * inner + there}

    def at_z(step):
        there = (z + step) % depth
        return there, {"seq": s + inner * (there // chan - half), "chan": there % chan}

    near = (2, 1, 3, 0)
    chip_steps = sorted(((x, y) for x in near for y in near), key=lambda xy: min(xy[0], 4 - xy[0]) + min(xy[1], 4 - xy[1]), reverse=True)
    plane_steps = [(x, y, other) for x, y in chip_steps for other in (1, 0)][:-1]
    same_steps = [(x, y, 0) for x, y in chip_steps[:-1]]
    z_steps = sorted(range(1, depth), key=lambda step: min(step, depth - step), reverse=True)
    partner = {"seq": s + inner * (1 - 2 * half)}
    twin = {"seq": s + 1 - 2 * core}

    barrier = pltpu.get_barrier_semaphore()

    def greet(device):
        pl.semaphore_signal(barrier, inc=1, device_id=device, device_id_type=MESH)

    for step in z_steps:
        greet(at_z(step)[1])
    loads = [
        pltpu.make_async_copy(src, dst, load_sem.at[i])
        for i, (src, dst) in enumerate(
            (
                (k_hbm, k_ref),
                (v_hbm, v_ref),
                (taps_hbm.at[0], column.at[z]),
                (q_hbm, q_ref),
                (bias_hbm, bias_ref),
                (groups_hbm, groups_ref),
                (offsets_hbm, offsets_ref),
            )
        )
    ]
    for load in loads:
        load.start()
    for step in plane_steps:
        greet(at_plane(step)[1])

    for load in loads:
        load.wait()
    for i in range(slabs):
        cols = slice(i * 128, (i + 1) * 128)
        turned = (k_ref[:, cols] * v_ref[:, cols]).T
        sent[i * inner : (i + 1) * inner] = turned.reshape(inner, chans, width)
    padded[:, :blocks] = jnp.zeros((chans, blocks, width), jnp.float32)
    padded[:, 2 * blocks - inner :] = jnp.zeros((chans, 2 * inner, width), jnp.float32)
    pl.semaphore_wait(barrier, plane - 1 + depth - 1)

    def copy_to(device, src, dst, send_sem, recv_sem):
        return pltpu.make_async_remote_copy(
            src_ref=src, dst_ref=dst, send_sem=send_sem, recv_sem=recv_sem, device_id=device, device_id_type=MESH
        )

    def tile_copy(i):
        other, device = at_plane(i)
        return copy_to(device, sent.at[other], tiles.at[p], tile_send, tile_recv)

    def table_copy(i):
        return copy_to(at_plane(i)[1], column, table.at[p % 2, p // 2], table_send, table_recv)

    def twin_copy():
        return copy_to(twin, table.at[p % 2], table.at[p % 2], twin_send, twin_recv)

    def foreign_copy(i):
        other, device = at_plane(i)
        rows = pl.ds(0, RAW)
        return copy_to(device, raw.at[other, rows], foreign.at[p, rows], foreign_send, foreign_recv)

    def back_copy(i, sub):
        other, device = at_plane(i)
        rows = pl.ds(sub * batch, batch)
        return copy_to(device, result.at[other, rows], returned.at[p, rows], back_send.at[sub], back_recv.at[sub])

    def tap_copy(i):
        return copy_to(at_z(i)[1], column.at[z], column.at[z], tap_send, tap_recv)

    def raw_copy(piece):
        rows = pl.ds(piece * (plane // RAW_PIECES), plane // RAW_PIECES)
        lanes = pl.ds(0, RAW)
        return copy_to(partner, sent.at[rows, lanes], raw.at[rows, lanes], raw_send.at[piece], raw_recv.at[piece])

    def far_copy(piece, count):
        rows, cols = pl.ds(piece * size, size), pl.ds(0, count)
        return copy_to(partner, mine.at[rows, cols], far.at[rows, cols], far_send.at[piece], far_recv.at[piece])

    def by_half(low, high, act):
        @pl.when(half == 0)
        def _():
            act(low)

        @pl.when(half == 1)
        def _():
            act(high)

    most = plane - inner

    def start_all(copy, steps):
        for step in steps:
            copy(step).start()

    def wait_bytes(ref, sem):
        pltpu.make_async_copy(ref, ref, sem).wait()

    def rows_of(c, x, side, last=0):
        for m in range(slabs):
            row = pl.multiple_of(blocks + m * 2 * inner + side * inner + (m == slabs - 1) * last, 8)
            padded[c, pl.ds(row, inner), :] = x[m * inner : (m + 1) * inner]

    start_all(tap_copy, z_steps)
    start_all(tile_copy, plane_steps)
    for piece in range(RAW_PIECES):
        raw_copy(piece).start()
    tiles[p] = sent[p]
    wait_bytes(tiles.at[pl.ds(0, plane - 1)], tile_recv)
    for piece in range(PIECES):
        for i in range(piece * size, (piece + 1) * size):
            x = tiles[:, RAW + i, :]
            mine[i] = x
            rows_of(RAW + i, x, half)
        by_half(plane, most, lambda count: far_copy(piece, count).start())
    for c in range(RAW):
        rows_of(c, tiles[:, c, :], half)
    wait_bytes(column.at[pl.ds(0, depth - 1)], tap_recv)
    start_all(table_copy, same_steps)
    own = pltpu.make_async_copy(column, table.at[p % 2, p // 2], own_sem)
    own.start()
    for piece in range(RAW_PIECES):
        raw_copy(piece).wait_recv()
    start_all(foreign_copy, plane_steps)
    foreign[p] = raw[p]
    own.wait()
    wait_bytes(table.at[0, pl.ds(0, chips - 1)], table_recv)
    twin_copy().start()
    row_at = lax.broadcasted_iota(jnp.int32, (width, width), 0)
    col_at = lax.broadcasted_iota(jnp.int32, (width, width), 1)
    same = col_at >= row_at
    none = jnp.zeros((width, width), jnp.bfloat16)

    def toeplitz(c, carry):
        group = groups_ref[p * chans + c]
        owner = group // chan
        there = (owner // inner) % 2 * chan + group % chan
        filt = table[owner % 2, (owner // (2 * inner)) * (inner // 2) + owner % inner // 2, there]
        for lag in range(lags):
            lines = jnp.broadcast_to(filt[lag : lag + 1], (width, width))
            rows = slice(lag * width, (lag + 1) * width)
            for part, held in zip(split(pltpu.roll(lines, 0, 1, stride=1, stride_axis=0)), (toep_hi, toep_lo)):
                held[c, rows, :width] = jnp.where(same, part, none)
                held[c, rows, width:] = jnp.where(same, none, part)
        return carry

    wait_bytes(table.at[0], twin_recv)
    lax.fori_loop(0, chans, toeplitz, 0, unroll=4)

    def convolve(c, x):
        rows_of(c, x, 1 - half, (1 - half) * inner)
        parts = [padded[c, pl.ds(blocks - offsets_ref[lag], blocks), :] for lag in range(lags)]
        hi, lo = split(jnp.concatenate(parts, axis=1))
        both = dot(jnp.concatenate([hi, lo], axis=0), toep_hi[c])
        y = both[:blocks] + both[blocks:] + dot(hi, toep_lo[c])
        tail = jnp.concatenate([jnp.zeros((1, width), jnp.float32), y[: blocks - 1, width:]], axis=0)
        total = y[:, :width] + tail
        for m in range(slabs):
            low = total[m * 2 * inner : m * 2 * inner + inner]
            high = total[m * 2 * inner + inner : (m + 1) * 2 * inner]
            result[m * inner : (m + 1) * inner, c, :] = jnp.where(half == 0, low, high)

    wait_bytes(foreign.at[pl.ds(0, plane - 1), pl.ds(0, RAW)], foreign_recv)
    for c in range(RAW):
        convolve(c, foreign[:, c, :])
        if (c + 1) % batch == 0:
            start_all(functools.partial(back_copy, sub=c // batch), plane_steps)
    for piece in range(PIECES):
        by_half(most, plane, lambda count: far_copy(piece, count).wait_recv())
        for i in range(piece * size, (piece + 1) * size):
            convolve(RAW + i, far[i])
            if (RAW + i + 1) % batch == 0 and RAW + i + 1 < chans:
                start_all(functools.partial(back_copy, sub=(RAW + i) // batch), plane_steps)
    start_all(functools.partial(back_copy, sub=BATCHES - 1), plane_steps)
    returned[p] = result[p]
    for piece in range(RAW_PIECES):
        raw_copy(piece).wait_send()
    for piece in range(PIECES):
        by_half(plane, most, lambda count: far_copy(piece, count).wait_send())
    wait_bytes(column.at[pl.ds(0, depth - 1)], tap_send)
    wait_bytes(sent.at[pl.ds(0, plane - 1)], tile_send)
    wait_bytes(foreign.at[pl.ds(0, plane - 1), pl.ds(0, RAW)], foreign_send)
    wait_bytes(table.at[0, pl.ds(0, chips - 1)], table_send)
    wait_bytes(table.at[0], twin_send)
    for sub in range(BATCHES):
        wait_bytes(result.at[pl.ds(0, plane - 1), pl.ds(0, batch)], back_send.at[sub])
    for sub in range(BATCHES):
        wait_bytes(returned.at[pl.ds(0, plane - 1), pl.ds(0, batch)], back_recv.at[sub])
    for i in range(slabs):
        cols = slice(i * 128, (i + 1) * 128)
        convolved = returned[i * inner : (i + 1) * inner].reshape(128, width).T
        gated = k_ref[:, cols] * v_ref[:, cols]
        o_ref[:, cols] = q_ref[:, cols] * (convolved + bias_ref[:, cols] * gated)


def local(q_proj, k_proj, v_proj, taps, skip_bias, group_index, offsets):
    width, chans = k_proj.shape
    lags = taps.shape[1]
    seq = lax.axis_size("seq")
    chan = lax.axis_size("chan")
    plane, depth = seq // 2, 2 * chan
    share = chans // plane
    hbm = pl.BlockSpec(memory_space=pltpu.HBM)
    f32, b16, dma = jnp.float32, jnp.bfloat16, pltpu.SemaphoreType.DMA
    return pl.pallas_call(
        kernel,
        out_shape=pltpu.VMEM((width, chans), f32),
        in_specs=[hbm] * 7,
        out_specs=pl.BlockSpec(memory_space=pltpu.VMEM),
        scratch_shapes=[
            pltpu.SMEM((chans,), jnp.int32),
            pltpu.SMEM((lags,), jnp.int32),
            pltpu.VMEM((width, chans), f32),
            pltpu.VMEM((width, chans), f32),
            pltpu.VMEM((width, chans), f32),
            pltpu.VMEM((1, chans), f32),
            pltpu.VMEM((plane, share, width), f32),
            pltpu.VMEM((plane, share, width), f32),
            pltpu.VMEM((plane, 8, width), f32),
            pltpu.VMEM((plane, 8, width), f32),
            pltpu.VMEM((share - RAW, plane, width), f32),
            pltpu.VMEM((share - RAW, plane, width), f32),
            pltpu.VMEM((share, 2 * seq + 8, width), f32),
            pltpu.VMEM((share, lags * width, 2 * width), b16),
            pltpu.VMEM((share, lags * width, 2 * width), b16),
            pltpu.VMEM((plane, share, width), f32),
            pltpu.VMEM((plane, share, width), f32),
            pltpu.VMEM((depth, lags, width), f32),
            pltpu.VMEM((2, plane // 2, depth, lags, width), f32),
            dma((7,)),
            dma(()),
            dma(()),
            dma((RAW_PIECES,)),
            dma((RAW_PIECES,)),
            dma(()),
            dma(()),
            dma((PIECES,)),
            dma((PIECES,)),
            dma(()),
            dma(()),
            dma(()),
            dma(()),
            dma(()),
            dma(()),
            dma(()),
            dma((BATCHES,)),
            dma((BATCHES,)),
        ],
        compiler_params=pltpu.CompilerParams(collective_id=0, has_side_effects=True, vmem_limit_bytes=58 << 20),
    )(group_index, offsets, q_proj, k_proj, v_proj, skip_bias[None, :], taps)


def solution(mesh):
    return jax.shard_map(
        local,
        mesh=mesh,
        in_specs=(
            P("seq", "chan"),
            P("seq", "chan"),
            P("seq", "chan"),
            P(("seq", "chan"), None, None),
            P("chan"),
            P("chan"),
            P(),
        ),
        out_specs=P("seq", "chan"),
        check_vma=False,
    )
```

```python
import functools

import jax
import jax.numpy as jnp
from jax import lax
from jax.experimental import pallas as pl
from jax.experimental.pallas import tpu as pltpu
from jax.sharding import PartitionSpec as P

MESH = pl.DeviceIdType.MESH
RAW = 4
RAW_PIECES = 1
PIECES = 4
BATCHES = 4


def split(x):
    hi = x.astype(jnp.bfloat16)
    lo = (x - hi.astype(jnp.float32)).astype(jnp.bfloat16)
    return hi, lo


def dot(a, b):
    return jnp.dot(a, b, preferred_element_type=jnp.float32)


def kernel(
    groups_hbm,
    offsets_hbm,
    q_hbm,
    k_hbm,
    v_hbm,
    bias_hbm,
    taps_hbm,
    o_ref,
    groups_ref,
    offsets_ref,
    q_ref,
    k_ref,
    v_ref,
    bias_ref,
    sent,
    tiles,
    raw,
    foreign,
    mine,
    far,
    padded,
    toep_hi,
    toep_lo,
    result,
    returned,
    column,
    table,
    load_sem,
    tile_send,
    tile_recv,
    raw_send,
    raw_recv,
    foreign_send,
    foreign_recv,
    far_send,
    far_recv,
    tap_send,
    tap_recv,
    table_send,
    table_recv,
    own_sem,
    twin_send,
    twin_recv,
    back_send,
    back_recv,
):
    width = k_ref.shape[0]
    lags = taps_hbm.shape[1]
    plane = tiles.shape[0]
    depth = column.shape[0]
    chans = padded.shape[0]
    chips = plane // 2
    batch = chans // BATCHES
    size = (chans - RAW) // PIECES
    inner = 8
    slabs = plane // inner
    chan = depth // 2
    blocks = 2 * plane
    s = lax.axis_index("seq")
    j = lax.axis_index("chan")
    half = (s // inner) % 2
    p = (s // (2 * inner)) * inner + s % inner
    z = half * chan + j

    mine_x, mine_y, core = p // inner, p // 2 % (inner // 2), p % 2

    def at_plane(step):
        right, up, other = step
        x, there = (mine_x + right) % slabs, (mine_y + up) % (inner // 2) * 2 + (core + other) % 2
        return x * inner + there, {"seq": x * 2 * inner + half * inner + there}

    def at_z(step):
        there = (z + step) % depth
        return there, {"seq": s + inner * (there // chan - half), "chan": there % chan}

    near = (2, 1, 3, 0)
    chip_steps = sorted(((x, y) for x in near for y in near), key=lambda xy: min(xy[0], 4 - xy[0]) + min(xy[1], 4 - xy[1]), reverse=True)
    plane_steps = [(x, y, other) for x, y in chip_steps for other in (1, 0)][:-1]
    same_steps = [(x, y, 0) for x, y in chip_steps[:-1]]
    z_steps = sorted(range(1, depth), key=lambda step: min(step, depth - step), reverse=True)
    partner = {"seq": s + inner * (1 - 2 * half)}
    twin = {"seq": s + 1 - 2 * core}

    barrier = pltpu.get_barrier_semaphore()

    def greet(device):
        pl.semaphore_signal(barrier, inc=1, device_id=device, device_id_type=MESH)

    for step in z_steps:
        greet(at_z(step)[1])
    loads = [
        pltpu.make_async_copy(src, dst, load_sem.at[i])
        for i, (src, dst) in enumerate(
            (
                (k_hbm, k_ref),
                (v_hbm, v_ref),
                (taps_hbm.at[0], column.at[z]),
                (q_hbm, q_ref),
                (bias_hbm, bias_ref),
                (groups_hbm, groups_ref),
                (offsets_hbm, offsets_ref),
            )
        )
    ]
    for load in loads:
        load.start()
    for step in plane_steps:
        greet(at_plane(step)[1])

    for load in loads:
        load.wait()
    for i in range(slabs):
        cols = slice(i * 128, (i + 1) * 128)
        turned = (k_ref[:, cols] * v_ref[:, cols]).T
        sent[i * inner : (i + 1) * inner] = turned.reshape(inner, chans, width)
    padded[:, :blocks] = jnp.zeros((chans, blocks, width), jnp.float32)
    padded[:, 2 * blocks - inner :] = jnp.zeros((chans, 2 * inner, width), jnp.float32)
    pl.semaphore_wait(barrier, plane - 1 + depth - 1)

    def copy_to(device, src, dst, send_sem, recv_sem):
        return pltpu.make_async_remote_copy(
            src_ref=src, dst_ref=dst, send_sem=send_sem, recv_sem=recv_sem, device_id=device, device_id_type=MESH
        )

    def tile_copy(i):
        other, device = at_plane(i)
        return copy_to(device, sent.at[other], tiles.at[p], tile_send, tile_recv)

    def table_copy(i):
        return copy_to(at_plane(i)[1], column, table.at[p % 2, p // 2], table_send, table_recv)

    def twin_copy():
        return copy_to(twin, table.at[p % 2], table.at[p % 2], twin_send, twin_recv)

    def foreign_copy(i):
        other, device = at_plane(i)
        rows = pl.ds(0, RAW)
        return copy_to(device, raw.at[other, rows], foreign.at[p, rows], foreign_send, foreign_recv)

    def back_copy(i, sub):
        other, device = at_plane(i)
        rows = pl.ds(sub * batch, batch)
        return copy_to(device, result.at[other, rows], returned.at[p, rows], back_send.at[sub], back_recv.at[sub])

    def tap_copy(i):
        return copy_to(at_z(i)[1], column.at[z], column.at[z], tap_send, tap_recv)

    def raw_copy(piece):
        rows = pl.ds(piece * (plane // RAW_PIECES), plane // RAW_PIECES)
        lanes = pl.ds(0, RAW)
        return copy_to(partner, sent.at[rows, lanes], raw.at[rows, lanes], raw_send.at[piece], raw_recv.at[piece])

    def far_copy(piece, count):
        rows, cols = pl.ds(piece * size, size), pl.ds(0, count)
        return copy_to(partner, mine.at[rows, cols], far.at[rows, cols], far_send.at[piece], far_recv.at[piece])

    def by_half(low, high, act):
        @pl.when(half == 0)
        def _():
            act(low)

        @pl.when(half == 1)
        def _():
            act(high)

    most = plane - inner

    def start_all(copy, steps):
        for step in steps:
            copy(step).start()

    def wait_bytes(ref, sem):
        pltpu.make_async_copy(ref, ref, sem).wait()

    def rows_of(c, x, side, last=0):
        for m in range(slabs):
            row = pl.multiple_of(blocks + m * 2 * inner + side * inner + (m == slabs - 1) * last, 8)
            padded[c, pl.ds(row, inner), :] = x[m * inner : (m + 1) * inner]

    start_all(tap_copy, z_steps)
    start_all(tile_copy, plane_steps)
    for piece in range(RAW_PIECES):
        raw_copy(piece).start()
    tiles[p] = sent[p]
    wait_bytes(tiles.at[pl.ds(0, plane - 1)], tile_recv)
    for piece in range(PIECES):
        for i in range(piece * size, (piece + 1) * size):
            x = tiles[:, RAW + i, :]
            mine[i] = x
            rows_of(RAW + i, x, half)

        @pl.when(half == 1)
        def _():
            far_copy(piece, most).start()

    for c in range(RAW):
        rows_of(c, tiles[:, c, :], half)
    wait_bytes(column.at[pl.ds(0, depth - 1)], tap_recv)
    start_all(table_copy, same_steps)
    own = pltpu.make_async_copy(column, table.at[p % 2, p // 2], own_sem)
    own.start()

    @pl.when(half == 0)
    def _():
        for piece in range(PIECES):
            far_copy(piece, plane).start()

    for piece in range(RAW_PIECES):
        raw_copy(piece).wait_recv()
    start_all(foreign_copy, plane_steps)
    foreign[p] = raw[p]
    own.wait()
    wait_bytes(table.at[0, pl.ds(0, chips - 1)], table_recv)
    twin_copy().start()
    row_at = lax.broadcasted_iota(jnp.int32, (width, width), 0)
    col_at = lax.broadcasted_iota(jnp.int32, (width, width), 1)
    same = col_at >= row_at
    none = jnp.zeros((width, width), jnp.bfloat16)

    def toeplitz(c, carry):
        group = groups_ref[p * chans + c]
        owner = group // chan
        there = (owner // inner) % 2 * chan + group % chan
        filt = table[owner % 2, (owner // (2 * inner)) * (inner // 2) + owner % inner // 2, there]
        for lag in range(lags):
            lines = jnp.broadcast_to(filt[lag : lag + 1], (width, width))
            rows = slice(lag * width, (lag + 1) * width)
            for part, held in zip(split(pltpu.roll(lines, 0, 1, stride=1, stride_axis=0)), (toep_hi, toep_lo)):
                held[c, rows, :width] = jnp.where(same, part, none)
                held[c, rows, width:] = jnp.where(same, none, part)
        return carry

    wait_bytes(table.at[0], twin_recv)
    lax.fori_loop(0, chans, toeplitz, 0, unroll=4)

    def convolve(c, x):
        rows_of(c, x, 1 - half, (1 - half) * inner)
        parts = [padded[c, pl.ds(blocks - offsets_ref[lag], blocks), :] for lag in range(lags)]
        hi, lo = split(jnp.concatenate(parts, axis=1))
        both = dot(jnp.concatenate([hi, lo], axis=0), toep_hi[c])
        y = both[:blocks] + both[blocks:] + dot(hi, toep_lo[c])
        tail = jnp.concatenate([jnp.zeros((1, width), jnp.float32), y[: blocks - 1, width:]], axis=0)
        total = y[:, :width] + tail
        for m in range(slabs):
            low = total[m * 2 * inner : m * 2 * inner + inner]
            high = total[m * 2 * inner + inner : (m + 1) * 2 * inner]
            result[m * inner : (m + 1) * inner, c, :] = jnp.where(half == 0, low, high)

    wait_bytes(foreign.at[pl.ds(0, plane - 1), pl.ds(0, RAW)], foreign_recv)
    for c in range(RAW):
        convolve(c, foreign[:, c, :])
        if (c + 1) % batch == 0:
            start_all(functools.partial(back_copy, sub=c // batch), plane_steps)
    for piece in range(PIECES):
        by_half(most, plane, lambda count: far_copy(piece, count).wait_recv())
        for i in range(piece * size, (piece + 1) * size):
            convolve(RAW + i, far[i])
            if (RAW + i + 1) % batch == 0 and RAW + i + 1 < chans:
                start_all(functools.partial(back_copy, sub=(RAW + i) // batch), plane_steps)
    start_all(functools.partial(back_copy, sub=BATCHES - 1), plane_steps)
    returned[p] = result[p]
    for piece in range(RAW_PIECES):
        raw_copy(piece).wait_send()
    for piece in range(PIECES):
        by_half(plane, most, lambda count: far_copy(piece, count).wait_send())
    wait_bytes(column.at[pl.ds(0, depth - 1)], tap_send)
    wait_bytes(sent.at[pl.ds(0, plane - 1)], tile_send)
    wait_bytes(foreign.at[pl.ds(0, plane - 1), pl.ds(0, RAW)], foreign_send)
    wait_bytes(table.at[0, pl.ds(0, chips - 1)], table_send)
    wait_bytes(table.at[0], twin_send)
    for sub in range(BATCHES):
        wait_bytes(result.at[pl.ds(0, plane - 1), pl.ds(0, batch)], back_send.at[sub])
    for sub in range(BATCHES):
        wait_bytes(returned.at[pl.ds(0, plane - 1), pl.ds(0, batch)], back_recv.at[sub])
    for i in range(slabs):
        cols = slice(i * 128, (i + 1) * 128)
        convolved = returned[i * inner : (i + 1) * inner].reshape(128, width).T
        gated = k_ref[:, cols] * v_ref[:, cols]
        o_ref[:, cols] = q_ref[:, cols] * (convolved + bias_ref[:, cols] * gated)


def local(q_proj, k_proj, v_proj, taps, skip_bias, group_index, offsets):
    width, chans = k_proj.shape
    lags = taps.shape[1]
    seq = lax.axis_size("seq")
    chan = lax.axis_size("chan")
    plane, depth = seq // 2, 2 * chan
    share = chans // plane
    hbm = pl.BlockSpec(memory_space=pltpu.HBM)
    f32, b16, dma = jnp.float32, jnp.bfloat16, pltpu.SemaphoreType.DMA
    return pl.pallas_call(
        kernel,
        out_shape=pltpu.VMEM((width, chans), f32),
        in_specs=[hbm] * 7,
        out_specs=pl.BlockSpec(memory_space=pltpu.VMEM),
        scratch_shapes=[
            pltpu.SMEM((chans,), jnp.int32),
            pltpu.SMEM((lags,), jnp.int32),
            pltpu.VMEM((width, chans), f32),
            pltpu.VMEM((width, chans), f32),
            pltpu.VMEM((width, chans), f32),
            pltpu.VMEM((1, chans), f32),
            pltpu.VMEM((plane, share, width), f32),
            pltpu.VMEM((plane, share, width), f32),
            pltpu.VMEM((plane, 8, width), f32),
            pltpu.VMEM((plane, 8, width), f32),
            pltpu.VMEM((share - RAW, plane, width), f32),
            pltpu.VMEM((share - RAW, plane, width), f32),
            pltpu.VMEM((share, 2 * seq + 8, width), f32),
            pltpu.VMEM((share, lags * width, 2 * width), b16),
            pltpu.VMEM((share, lags * width, 2 * width), b16),
            pltpu.VMEM((plane, share, width), f32),
            pltpu.VMEM((plane, share, width), f32),
            pltpu.VMEM((depth, lags, width), f32),
            pltpu.VMEM((2, plane // 2, depth, lags, width), f32),
            dma((7,)),
            dma(()),
            dma(()),
            dma((RAW_PIECES,)),
            dma((RAW_PIECES,)),
            dma(()),
            dma(()),
            dma((PIECES,)),
            dma((PIECES,)),
            dma(()),
            dma(()),
            dma(()),
            dma(()),
            dma(()),
            dma(()),
            dma(()),
            dma((BATCHES,)),
            dma((BATCHES,)),
        ],
        compiler_params=pltpu.CompilerParams(collective_id=0, has_side_effects=True, vmem_limit_bytes=58 << 20),
    )(group_index, offsets, q_proj, k_proj, v_proj, skip_bias[None, :], taps)


def solution(mesh):
    return jax.shard_map(
        local,
        mesh=mesh,
        in_specs=(
            P("seq", "chan"),
            P("seq", "chan"),
            P("seq", "chan"),
            P(("seq", "chan"), None, None),
            P("chan"),
            P("chan"),
            P(),
        ),
        out_specs=P("seq", "chan"),
        check_vma=False,
    )
```

```python
import functools

import jax
import jax.numpy as jnp
from jax import lax
from jax.experimental import pallas as pl
from jax.experimental.pallas import tpu as pltpu
from jax.sharding import PartitionSpec as P

MESH = pl.DeviceIdType.MESH
RAW = 4
RAW_PIECES = 1
PIECES = 6
BATCHES = 4


def split(x):
    hi = x.astype(jnp.bfloat16)
    lo = (x - hi.astype(jnp.float32)).astype(jnp.bfloat16)
    return hi, lo


def dot(a, b):
    return jnp.dot(a, b, preferred_element_type=jnp.float32)


def kernel(
    groups_hbm,
    offsets_hbm,
    q_hbm,
    k_hbm,
    v_hbm,
    bias_hbm,
    taps_hbm,
    o_ref,
    groups_ref,
    offsets_ref,
    q_ref,
    k_ref,
    v_ref,
    bias_ref,
    sent,
    tiles,
    raw,
    foreign,
    mine,
    far,
    padded,
    toep_hi,
    toep_lo,
    result,
    returned,
    column,
    table,
    load_sem,
    tile_send,
    tile_recv,
    raw_send,
    raw_recv,
    foreign_send,
    foreign_recv,
    far_send,
    far_recv,
    tap_send,
    tap_recv,
    table_send,
    table_recv,
    own_sem,
    twin_send,
    twin_recv,
    back_send,
    back_recv,
):
    width = k_ref.shape[0]
    lags = taps_hbm.shape[1]
    plane = tiles.shape[0]
    depth = column.shape[0]
    chans = padded.shape[0]
    chips = plane // 2
    batch = chans // BATCHES
    size = (chans - RAW) // PIECES
    inner = 8
    slabs = plane // inner
    chan = depth // 2
    blocks = 2 * plane
    s = lax.axis_index("seq")
    j = lax.axis_index("chan")
    half = (s // inner) % 2
    p = (s // (2 * inner)) * inner + s % inner
    z = half * chan + j

    mine_x, mine_y, core = p // inner, p // 2 % (inner // 2), p % 2

    def at_plane(step):
        right, up, other = step
        x, there = (mine_x + right) % slabs, (mine_y + up) % (inner // 2) * 2 + (core + other) % 2
        return x * inner + there, {"seq": x * 2 * inner + half * inner + there}

    def at_z(step):
        there = (z + step) % depth
        return there, {"seq": s + inner * (there // chan - half), "chan": there % chan}

    near = (2, 1, 3, 0)
    chip_steps = sorted(((x, y) for x in near for y in near), key=lambda xy: min(xy[0], 4 - xy[0]) + min(xy[1], 4 - xy[1]), reverse=True)
    plane_steps = [(x, y, other) for x, y in chip_steps for other in (1, 0)][:-1]
    same_steps = [(x, y, 0) for x, y in chip_steps[:-1]]
    z_steps = sorted(range(1, depth), key=lambda step: min(step, depth - step), reverse=True)
    partner = {"seq": s + inner * (1 - 2 * half)}
    twin = {"seq": s + 1 - 2 * core}

    barrier = pltpu.get_barrier_semaphore()

    def greet(device):
        pl.semaphore_signal(barrier, inc=1, device_id=device, device_id_type=MESH)

    for step in z_steps:
        greet(at_z(step)[1])
    loads = [
        pltpu.make_async_copy(src, dst, load_sem.at[i])
        for i, (src, dst) in enumerate(
            (
                (k_hbm, k_ref),
                (v_hbm, v_ref),
                (taps_hbm.at[0], column.at[z]),
                (q_hbm, q_ref),
                (bias_hbm, bias_ref),
                (groups_hbm, groups_ref),
                (offsets_hbm, offsets_ref),
            )
        )
    ]
    for load in loads:
        load.start()
    for step in plane_steps:
        greet(at_plane(step)[1])

    for load in loads:
        load.wait()
    for i in range(slabs):
        cols = slice(i * 128, (i + 1) * 128)
        turned = (k_ref[:, cols] * v_ref[:, cols]).T
        sent[i * inner : (i + 1) * inner] = turned.reshape(inner, chans, width)
    padded[:, :blocks] = jnp.zeros((chans, blocks, width), jnp.float32)
    padded[:, 2 * blocks - inner :] = jnp.zeros((chans, 2 * inner, width), jnp.float32)
    pl.semaphore_wait(barrier, plane - 1 + depth - 1)

    def copy_to(device, src, dst, send_sem, recv_sem):
        return pltpu.make_async_remote_copy(
            src_ref=src, dst_ref=dst, send_sem=send_sem, recv_sem=recv_sem, device_id=device, device_id_type=MESH
        )

    def tile_copy(i):
        other, device = at_plane(i)
        return copy_to(device, sent.at[other], tiles.at[p], tile_send, tile_recv)

    def table_copy(i):
        return copy_to(at_plane(i)[1], column, table.at[p % 2, p // 2], table_send, table_recv)

    def twin_copy():
        return copy_to(twin, table.at[p % 2], table.at[p % 2], twin_send, twin_recv)

    def foreign_copy(i):
        other, device = at_plane(i)
        rows = pl.ds(0, RAW)
        return copy_to(device, raw.at[other, rows], foreign.at[p, rows], foreign_send, foreign_recv)

    def back_copy(i, sub):
        other, device = at_plane(i)
        rows = pl.ds(sub * batch, batch)
        return copy_to(device, result.at[other, rows], returned.at[p, rows], back_send.at[sub], back_recv.at[sub])

    def tap_copy(i):
        return copy_to(at_z(i)[1], column.at[z], column.at[z], tap_send, tap_recv)

    def raw_copy(piece):
        rows = pl.ds(piece * (plane // RAW_PIECES), plane // RAW_PIECES)
        lanes = pl.ds(0, RAW)
        return copy_to(partner, sent.at[rows, lanes], raw.at[rows, lanes], raw_send.at[piece], raw_recv.at[piece])

    def far_copy(piece, count):
        rows, cols = pl.ds(piece * size, size), pl.ds(0, count)
        return copy_to(partner, mine.at[rows, cols], far.at[rows, cols], far_send.at[piece], far_recv.at[piece])

    def by_half(low, high, act):
        @pl.when(half == 0)
        def _():
            act(low)

        @pl.when(half == 1)
        def _():
            act(high)

    most = plane - inner

    def start_all(copy, steps):
        for step in steps:
            copy(step).start()

    def wait_bytes(ref, sem):
        pltpu.make_async_copy(ref, ref, sem).wait()

    def rows_of(c, x, side, last=0):
        for m in range(slabs):
            row = pl.multiple_of(blocks + m * 2 * inner + side * inner + (m == slabs - 1) * last, 8)
            padded[c, pl.ds(row, inner), :] = x[m * inner : (m + 1) * inner]

    start_all(tap_copy, z_steps)
    start_all(tile_copy, plane_steps)
    for piece in range(RAW_PIECES):
        raw_copy(piece).start()
    tiles[p] = sent[p]
    wait_bytes(tiles.at[pl.ds(0, plane - 1)], tile_recv)
    for piece in range(PIECES):
        for i in range(piece * size, (piece + 1) * size):
            x = tiles[:, RAW + i, :]
            mine[i] = x
            rows_of(RAW + i, x, half)

        @pl.when(half == 1)
        def _():
            far_copy(piece, most).start()

    for c in range(RAW):
        rows_of(c, tiles[:, c, :], half)
    wait_bytes(column.at[pl.ds(0, depth - 1)], tap_recv)
    start_all(table_copy, same_steps)
    own = pltpu.make_async_copy(column, table.at[p % 2, p // 2], own_sem)
    own.start()

    @pl.when(half == 0)
    def _():
        for piece in range(PIECES):
            far_copy(piece, plane).start()

    for piece in range(RAW_PIECES):
        raw_copy(piece).wait_recv()
    start_all(foreign_copy, plane_steps)
    foreign[p] = raw[p]
    own.wait()
    wait_bytes(table.at[0, pl.ds(0, chips - 1)], table_recv)
    twin_copy().start()
    row_at = lax.broadcasted_iota(jnp.int32, (width, width), 0)
    col_at = lax.broadcasted_iota(jnp.int32, (width, width), 1)
    same = col_at >= row_at
    none = jnp.zeros((width, width), jnp.bfloat16)

    def toeplitz(c, carry):
        group = groups_ref[p * chans + c]
        owner = group // chan
        there = (owner // inner) % 2 * chan + group % chan
        filt = table[owner % 2, (owner // (2 * inner)) * (inner // 2) + owner % inner // 2, there]
        for lag in range(lags):
            lines = jnp.broadcast_to(filt[lag : lag + 1], (width, width))
            rows = slice(lag * width, (lag + 1) * width)
            for part, held in zip(split(pltpu.roll(lines, 0, 1, stride=1, stride_axis=0)), (toep_hi, toep_lo)):
                held[c, rows, :width] = jnp.where(same, part, none)
                held[c, rows, width:] = jnp.where(same, none, part)
        return carry

    wait_bytes(table.at[0], twin_recv)
    lax.fori_loop(0, chans, toeplitz, 0, unroll=4)

    def convolve(c, x):
        rows_of(c, x, 1 - half, (1 - half) * inner)
        parts = [padded[c, pl.ds(blocks - offsets_ref[lag], blocks), :] for lag in range(lags)]
        hi, lo = split(jnp.concatenate(parts, axis=1))
        both = dot(jnp.concatenate([hi, lo], axis=0), toep_hi[c])
        y = both[:blocks] + both[blocks:] + dot(hi, toep_lo[c])
        tail = jnp.concatenate([jnp.zeros((1, width), jnp.float32), y[: blocks - 1, width:]], axis=0)
        total = y[:, :width] + tail
        for m in range(slabs):
            low = total[m * 2 * inner : m * 2 * inner + inner]
            high = total[m * 2 * inner + inner : (m + 1) * 2 * inner]
            result[m * inner : (m + 1) * inner, c, :] = jnp.where(half == 0, low, high)

    def give_back(c):
        if (c + 1) % batch == 0 and c + 1 < chans:
            start_all(functools.partial(back_copy, sub=c // batch), plane_steps)

    for piece in range(PIECES):
        if piece == 4:
            wait_bytes(foreign.at[pl.ds(0, plane - 1), pl.ds(0, RAW)], foreign_recv)
            for c in range(RAW):
                convolve(c, foreign[:, c, :])
                give_back(c)
        by_half(most, plane, lambda count: far_copy(piece, count).wait_recv())
        for c in range(RAW + piece * size, RAW + (piece + 1) * size):
            convolve(c, far[c - RAW])
            give_back(c)
    start_all(functools.partial(back_copy, sub=BATCHES - 1), plane_steps)
    returned[p] = result[p]
    for piece in range(RAW_PIECES):
        raw_copy(piece).wait_send()
    for piece in range(PIECES):
        by_half(plane, most, lambda count: far_copy(piece, count).wait_send())
    wait_bytes(column.at[pl.ds(0, depth - 1)], tap_send)
    wait_bytes(sent.at[pl.ds(0, plane - 1)], tile_send)
    wait_bytes(foreign.at[pl.ds(0, plane - 1), pl.ds(0, RAW)], foreign_send)
    wait_bytes(table.at[0, pl.ds(0, chips - 1)], table_send)
    wait_bytes(table.at[0], twin_send)
    for sub in range(BATCHES):
        wait_bytes(result.at[pl.ds(0, plane - 1), pl.ds(0, batch)], back_send.at[sub])
    for sub in range(BATCHES):
        wait_bytes(returned.at[pl.ds(0, plane - 1), pl.ds(0, batch)], back_recv.at[sub])
    for i in range(slabs):
        cols = slice(i * 128, (i + 1) * 128)
        convolved = returned[i * inner : (i + 1) * inner].reshape(128, width).T
        gated = k_ref[:, cols] * v_ref[:, cols]
        o_ref[:, cols] = q_ref[:, cols] * (convolved + bias_ref[:, cols] * gated)


def local(q_proj, k_proj, v_proj, taps, skip_bias, group_index, offsets):
    width, chans = k_proj.shape
    lags = taps.shape[1]
    seq = lax.axis_size("seq")
    chan = lax.axis_size("chan")
    plane, depth = seq // 2, 2 * chan
    share = chans // plane
    hbm = pl.BlockSpec(memory_space=pltpu.HBM)
    f32, b16, dma = jnp.float32, jnp.bfloat16, pltpu.SemaphoreType.DMA
    return pl.pallas_call(
        kernel,
        out_shape=pltpu.VMEM((width, chans), f32),
        in_specs=[hbm] * 7,
        out_specs=pl.BlockSpec(memory_space=pltpu.VMEM),
        scratch_shapes=[
            pltpu.SMEM((chans,), jnp.int32),
            pltpu.SMEM((lags,), jnp.int32),
            pltpu.VMEM((width, chans), f32),
            pltpu.VMEM((width, chans), f32),
            pltpu.VMEM((width, chans), f32),
            pltpu.VMEM((1, chans), f32),
            pltpu.VMEM((plane, share, width), f32),
            pltpu.VMEM((plane, share, width), f32),
            pltpu.VMEM((plane, 8, width), f32),
            pltpu.VMEM((plane, 8, width), f32),
            pltpu.VMEM((share - RAW, plane, width), f32),
            pltpu.VMEM((share - RAW, plane, width), f32),
            pltpu.VMEM((share, 2 * seq + 8, width), f32),
            pltpu.VMEM((share, lags * width, 2 * width), b16),
            pltpu.VMEM((share, lags * width, 2 * width), b16),
            pltpu.VMEM((plane, share, width), f32),
            pltpu.VMEM((plane, share, width), f32),
            pltpu.VMEM((depth, lags, width), f32),
            pltpu.VMEM((2, plane // 2, depth, lags, width), f32),
            dma((7,)),
            dma(()),
            dma(()),
            dma((RAW_PIECES,)),
            dma((RAW_PIECES,)),
            dma(()),
            dma(()),
            dma((PIECES,)),
            dma((PIECES,)),
            dma(()),
            dma(()),
            dma(()),
            dma(()),
            dma(()),
            dma(()),
            dma(()),
            dma((BATCHES,)),
            dma((BATCHES,)),
        ],
        compiler_params=pltpu.CompilerParams(collective_id=0, has_side_effects=True, vmem_limit_bytes=58 << 20),
    )(group_index, offsets, q_proj, k_proj, v_proj, skip_bias[None, :], taps)


def solution(mesh):
    return jax.shard_map(
        local,
        mesh=mesh,
        in_specs=(
            P("seq", "chan"),
            P("seq", "chan"),
            P("seq", "chan"),
            P(("seq", "chan"), None, None),
            P("chan"),
            P("chan"),
            P(),
        ),
        out_specs=P("seq", "chan"),
        check_vma=False,
    )
```
